256 devices in a mesh: row: 16 (over z_hi, x, core), col: 16 (over z_lo, y).
Axes of the slice: x: 4, y: 4, z: 8 (z_hi: 2, z_lo: 4; z = z_hi * 4 + z_lo), core: 2. Of those that a mesh axis runs over, the one named last changes fastest.
Arguments:
- orbitals: bfloat16 [1024, 16384], P(('row', 'col')), may hold values from -0.09375 to 0.09375
- gradient: bfloat16 [1024, 16384], P(('row', 'col')), may hold values from -6 to 6
- stored: float32 [16384, 16384], P('row', 'col'), as said below
Outputs:
- projected: bfloat16 [1024, 16384], P(('row', 'col'))
The draws below stay inside these ranges and needn't reach their ends.
Inputs may be any that keep to these rules, and one draw needn't show every extreme that they name: stored is exactly symmetric: stored[i, j] equals stored[j, i].
All inputs are finite; a program needn't handle non-finite values.
Results may differ from the reference program's by a relative error of at most 0.0034.
Values may be sent and summed in bfloat16 or wider, within the bound.
No kernel may reach another device: no remote copies, remote signals or barrier semaphores. Data moves between devices by JAX's collectives and lax.ppermute only.
A program may use at most 64 MiB of HBM per device.

```python
import math
import jax
import jax.numpy as jnp
from jax import lax

NORB = 16384
NPW = 1024


def draw_stored(key, part):
    base = jax.random.normal(key, (NORB, NORB), jnp.float32)
    return (base + base.T) * 0.18


def steps_of(key, extent, cuts, smallest, largest):
    gain = 1.0
    for axis_at, blocks in cuts:
        steps = jax.random.uniform(jax.random.fold_in(jax.random.fold_in(key, 6), axis_at), (blocks,), jnp.float32, smallest / len(cuts), largest / len(cuts))
        gain = gain * jnp.repeat(jnp.exp(steps), extent[axis_at] // blocks).reshape((-1,) + (1,) * (len(extent) - 1 - axis_at))
    return gain


def gaussian(key, extent, deviation, most, cuts=(), kind=jnp.bfloat16):
    factor_of = steps_of(key, extent, cuts, -0.22, 0.18) if cuts else 1.0
    entries = jax.random.normal(key, extent, jnp.float32) * deviation * factor_of
    return jnp.minimum(jnp.maximum(entries, -most), most).astype(kind)


def setup_inputs(seed: int = 0) -> dict:
    seeds = jax.random.split(jax.random.key(seed), 4)
    return {
        "orbitals": gaussian(seeds[0], (NPW, NORB), ((NPW * NORB) ** -0.25), 0.09375, ((0, 256),)),
        "gradient": gaussian(seeds[1], (NPW, NORB), 1.0, 6.0, ((0, 256),)),
        "stored": draw_stored(jax.random.fold_in(seeds[3], 71), 0),
    }


def reference(orbitals, gradient, stored):
    width = math.gcd(NORB, 1024)
    count = NORB // width

    def column_block(index):
        start = (index * width).astype(jnp.int32)
        orb_cols = lax.dynamic_slice_in_dim(orbitals, start, width, 1)
        grad_cols = lax.dynamic_slice_in_dim(gradient, start, width, 1)
        kept_cols = lax.dynamic_slice_in_dim(stored, start, width, 1)
        half_cols = (0.5 * jnp.dot(orbitals.T, grad_cols, preferred_element_type=jnp.float32) + 0.5 * kept_cols).astype(jnp.bfloat16)
        half_rows = (0.5 * jnp.dot(gradient.T, orb_cols, preferred_element_type=jnp.float32) + 0.5 * kept_cols).astype(jnp.bfloat16)
        correction = jnp.dot(orbitals, half_cols, preferred_element_type=jnp.float32) + jnp.dot(orbitals, half_rows, preferred_element_type=jnp.float32)
        return (grad_cols.astype(jnp.float32) - correction).astype(jnp.bfloat16)

    blocks = lax.map(column_block, jnp.arange(count, dtype=jnp.int32))
    return jnp.transpose(blocks, (1, 0, 2)).reshape(NPW, NORB)
```

```python
import jax
import jax.numpy as jnp
from jax import lax
from jax.sharding import Mesh, PartitionSpec as P

AXES = ("zh", "x", "core", "zl", "y")
SIZES = {"zh": 2, "x": 4, "core": 2, "zl": 4, "y": 4}
F32, BF16 = jnp.float32, jnp.bfloat16


def shift(value, axis, step):
    n = SIZES[axis]
    return lax.ppermute(value, axis, [(i, (i + step) % n) for i in range(n)])


def partner(value, axis, bits):
    return lax.ppermute(value, axis, [(i, i ^ bits) for i in range(SIZES[axis])])


def pick(value, index, dim=0):
    return lax.dynamic_index_in_dim(value, index, dim, keepdims=False)


def place(whole, piece, index):
    return lax.dynamic_update_index_in_dim(whole, piece, index, 0)


def exchange(pieces, axis):
    me = lax.axis_index(axis)
    got = [partner(pick(pieces, me ^ d), axis, d) for d in range(1, SIZES[axis])]
    for d, piece in enumerate(got, 1):
        pieces = place(pieces, piece, me ^ d)
    return pieces


def gather(block, axis):
    me = lax.axis_index(axis)
    n = SIZES[axis]
    whole = place(jnp.zeros((n,) + block.shape, block.dtype), block, me)
    got = [shift(block, axis, d) for d in range(1, n)]
    for d, piece in enumerate(got, 1):
        whole = place(whole, piece, (me - d) % n)
    return whole


def gather_ring(block, axis):
    me = lax.axis_index(axis)
    half = block.shape[0] // 2
    left, right = shift(block, axis, 1), shift(block, axis, -1)
    far = jnp.concatenate([shift(left[:half], axis, 1), shift(right[half:], axis, -1)])
    whole = place(jnp.zeros((4,) + block.shape, block.dtype), block, me)
    whole = place(whole, left, (me + 3) % 4)
    whole = place(whole, right, (me + 1) % 4)
    return place(whole, far, (me + 2) % 4)


def reduce_to(pieces, axis, wire):
    me = lax.axis_index(axis)
    got = [partner(pick(pieces, me ^ d).astype(wire), axis, d) for d in range(1, SIZES[axis])]
    return sum((g.astype(F32) for g in got), pick(pieces, me))


def dot(left, right, dims):
    return lax.dot_general(left, right, (dims, ((), ())), preferred_element_type=F32)


def body(orbitals, gradient, stored):
    k, n = orbitals.shape
    w, hw = n // 16, n // 32
    core = lax.axis_index("core")

    own = jnp.stack([orbitals, gradient])
    sibling = partner(own, "core", 1)
    both = jnp.where(core == 0, jnp.concatenate([own, sibling], 1), jnp.concatenate([sibling, own], 1))
    rows = 2 * k

    to_r = pick(both.reshape(2, rows, 2, 4, 2, w), core, 4).transpose(3, 2, 0, 1, 4)
    to_c = pick(both.reshape(2, rows, 4, 4, 2, hw), core, 4).transpose(3, 2, 0, 1, 4)
    part_r = exchange(jnp.swapaxes(exchange(to_r, "x"), 0, 1), "zh")
    part_c = exchange(jnp.swapaxes(exchange(to_c, "y"), 0, 1), "zl")

    x_r = part_r[:, :, 0].reshape(8 * rows, w)
    x_r = gather_ring(gather(x_r, "zl"), "y").reshape(128 * rows, w)
    panel = gather_ring(gather(part_c, "zh"), "x")

    pairs = dot(x_r, part_r.reshape(16 * rows, w), ((1,), (1,)))
    pairs = reduce_to(pairs.reshape(2, 64 * rows, 16 * rows), "core", F32)
    pairs = pairs.reshape(2, 4, 2, 4, rows, 16 * rows)
    pairs = reduce_to(pairs.transpose(3, 2, 0, 1, 4, 5), "x", F32)
    pairs = reduce_to(pairs, "zh", F32)
    pairs = gather(gather(pairs, "zl"), "y")
    pairs = gather(pairs, "core")
    pairs = pairs.reshape(2, 16, 8 * rows, 16 * rows).transpose(0, 2, 1, 3).reshape(16 * rows, -1)

    tiles = dot(x_r, stored.astype(BF16), ((1,), (0,)))
    tiles = reduce_to(tiles.reshape(128 * rows, 2, hw).transpose(1, 0, 2), "core", F32)
    tiles = tiles.reshape(4, 4, 2, 4, rows, hw)
    tiles = reduce_to(tiles.transpose(3, 2, 0, 1, 4, 5), "x", BF16)
    tiles = reduce_to(tiles, "zh", F32)

    other = panel[:, :, :, :, ::-1].transpose(3, 2, 1, 0, 4, 5, 6).reshape(-1, hw)
    high = lax.reduce_precision(pairs, 8, 7)
    low = pairs - high
    mixed = dot(high.astype(BF16), other, ((1,), (0,))) + dot(low.astype(BF16), other, ((1,), (0,)))

    mine = part_c[:, :, 1].transpose(1, 0, 2, 3).astype(F32)
    result = (mine - (0.5 * mixed.reshape(mine.shape) + tiles)).astype(BF16)
    result = lax.all_to_all(
        result.transpose(1, 0, 2, 3).reshape(16, rows, hw), ("zl", "y"), split_axis=0, concat_axis=0, tiled=True
    )
    result = result.reshape(16, 2, k, hw)
    kept, got = pick(result, core, 1), partner(pick(result, 1 - core, 1), "core", 1)
    halves = jnp.where(core == 0, jnp.stack([kept, got]), jnp.stack([got, kept]))
    return halves.transpose(2, 1, 0, 3).reshape(k, n)


def solution(mesh):
    fine = Mesh(mesh.devices.reshape(tuple(SIZES.values())), AXES)
    return jax.shard_map(
        body,
        mesh=fine,
        in_specs=(P(AXES, None), P(AXES, None), P(("zh", "x", "core"), ("zl", "y"))),
        out_specs=P(AXES, None),
        check_vma=False,
    )
```

```python
import jax
import jax.numpy as jnp
from jax import lax
from jax.sharding import Mesh, PartitionSpec as P

AXES = ("zh", "x", "core", "zl", "y")
SIZES = {"zh": 2, "x": 4, "core": 2, "zl": 4, "y": 4}
F32, BF16 = jnp.float32, jnp.bfloat16


def shift(value, axis, step):
    n = SIZES[axis]
    return lax.ppermute(value, axis, [(i, (i + step) % n) for i in range(n)])


def partner(value, axis, bits):
    return lax.ppermute(value, axis, [(i, i ^ bits) for i in range(SIZES[axis])])


def pick(value, index, dim=0):
    return lax.dynamic_index_in_dim(value, index, dim, keepdims=False)


def place(whole, piece, index):
    return lax.dynamic_update_index_in_dim(whole, piece, index, 0)


def exchange(pieces, axis):
    me = lax.axis_index(axis)
    got = [partner(pick(pieces, me ^ d), axis, d) for d in range(1, SIZES[axis])]
    for d, piece in enumerate(got, 1):
        pieces = place(pieces, piece, me ^ d)
    return pieces


def gather(block, axis):
    me = lax.axis_index(axis)
    n = SIZES[axis]
    whole = place(jnp.zeros((n,) + block.shape, block.dtype), block, me)
    got = [shift(block, axis, d) for d in range(1, n)]
    for d, piece in enumerate(got, 1):
        whole = place(whole, piece, (me - d) % n)
    return whole


def gather_ring(block, axis):
    me = lax.axis_index(axis)
    half = block.shape[0] // 2
    left, right = shift(block, axis, 1), shift(block, axis, -1)
    far = jnp.concatenate([shift(left[:half], axis, 1), shift(right[half:], axis, -1)])
    whole = place(jnp.zeros((4,) + block.shape, block.dtype), block, me)
    whole = place(whole, left, (me + 3) % 4)
    whole = place(whole, right, (me + 1) % 4)
    return place(whole, far, (me + 2) % 4)


def reduce_to(pieces, axis, wire):
    me = lax.axis_index(axis)
    got = [partner(pick(pieces, me ^ d).astype(wire), axis, d) for d in range(1, SIZES[axis])]
    return sum((g.astype(F32) for g in got), pick(pieces, me))


def dot(left, right, dims):
    return lax.dot_general(left, right, (dims, ((), ())), preferred_element_type=F32)


def body(orbitals, gradient, stored):
    k, n = orbitals.shape
    w, hw = n // 16, n // 32
    core = lax.axis_index("core")

    own = jnp.stack([orbitals, gradient])
    sibling = partner(own, "core", 1)
    both = jnp.where(core == 0, jnp.concatenate([own, sibling], 1), jnp.concatenate([sibling, own], 1))
    rows = 2 * k

    to_r = pick(both.reshape(2, rows, 2, 4, 2, w), core, 4).transpose(3, 2, 0, 1, 4)
    to_c = pick(both[::-1].reshape(2, rows, 4, 4, 2, hw), core, 4).transpose(3, 2, 0, 1, 4)
    part_r = exchange(jnp.swapaxes(exchange(to_r, "x"), 0, 1), "zh")
    part_c = exchange(jnp.swapaxes(exchange(to_c, "y"), 0, 1), "zl")

    panel_r = gather_ring(gather(part_r.reshape(16 * rows, w), "zl"), "y")
    panel_c = gather_ring(gather(part_c, "zh"), "x")
    panel_c = panel_c.transpose(3, 2, 1, 0, 4, 5, 6).reshape(-1, hw)
    panel_d = partner(panel_c, "core", 1)

    panel_r = panel_r.reshape(256 * rows, w)
    x_r = panel_r.reshape(128, 2, rows, w)[:, 0].reshape(128 * rows, w)
    split = stored.reshape(w, 2, hw)

    def share(panel, which):
        tile = 0.5 * dot(panel_r, panel, ((0,), (0,))) + pick(split, which, 1)
        return dot(x_r, tile.astype(BF16), ((1,), (0,)))

    away = partner(share(panel_d, 1 - core), "core", 1)
    total = share(panel_c, core) + away
    total = total.reshape(4, 4, 2, 4, rows, hw)
    total = reduce_to(total.transpose(3, 2, 0, 1, 4, 5), "x", BF16)
    total = reduce_to(total, "zh", F32)

    mine = part_c[:, :, 0].transpose(1, 0, 2, 3).astype(F32)
    result = (mine - total).astype(BF16)
    result = lax.all_to_all(
        result.transpose(1, 0, 2, 3).reshape(16, rows, hw), ("zl", "y"), split_axis=0, concat_axis=0, tiled=True
    )
    result = result.reshape(16, 2, k, hw)
    kept, got = pick(result, core, 1), partner(pick(result, 1 - core, 1), "core", 1)
    halves = jnp.where(core == 0, jnp.stack([kept, got]), jnp.stack([got, kept]))
    return halves.transpose(2, 1, 0, 3).reshape(k, n)


def solution(mesh):
    fine = Mesh(mesh.devices.reshape(tuple(SIZES.values())), AXES)
    return jax.shard_map(
        body,
        mesh=fine,
        in_specs=(P(AXES, None), P(AXES, None), P(("zh", "x", "core"), ("zl", "y"))),
        out_specs=P(AXES, None),
        check_vma=False,
    )
```

```python
import jax
import jax.numpy as jnp
from jax import lax
from jax.experimental import pallas as pl
from jax.experimental.pallas import tpu as pltpu
from jax.sharding import Mesh, PartitionSpec as P

AXES = ("zh", "x", "core", "zl", "y")
SIZES = {"zh": 2, "x": 4, "core": 2, "zl": 4, "y": 4}
F32, BF16 = jnp.float32, jnp.bfloat16


def shift(value, axis, step):
    n = SIZES[axis]
    return lax.ppermute(value, axis, [(i, (i + step) % n) for i in range(n)])


def pick(value, index, dim=0):
    return lax.dynamic_index_in_dim(value, index, dim, keepdims=False)


def exchange(pieces, axis, dim):
    n = SIZES[axis]
    me = lax.axis_index(axis)
    sent = [pick(pieces, (me + d) % n, dim) for d in range(n)]
    return jnp.stack([sent[0]] + [shift(sent[d], axis, d) for d in range(1, n)])


def gather(block, axis):
    return [block] + [shift(block, axis, d) for d in range(1, SIZES[axis])]


def gather_ring(block, axis):
    half = block.shape[0] // 2
    left, right = shift(block, axis, 1), shift(block, axis, -1)
    return block, left, shift(left[:half], axis, 1), shift(right[half:], axis, -1), right


def dot(left, right, dims):
    return lax.dot_general(left, right, (dims, ((), ())), preferred_element_type=F32)


def early_kernel(a0, a1, a3, cols, out):
    total = None
    for a, j in ((a0, 0), (a1, 1), (a3, 3)):
        term = dot(flat(a[...]), flat(cols[j]), ((0,), (0,)))
        total = term if total is None else total + term
    out[...] = total


def share_kernel(a0, a1, a2, a2b, a3, e0, e1, e2, e3, cols, early, kept, out):
    wa = early.shape[0]
    rows = a0.shape[1] // 2
    main = early[...]
    main += dot(flat(a2[...]), flat(cols[2, :2]), ((0,), (0,)))
    main += dot(flat(a2b[...]), flat(cols[2, 2:]), ((0,), (0,)))
    main = (0.5 * main + kept[:wa]).astype(BF16)
    side = None
    for d, e in enumerate((e0, e1, e2, e3)):
        term = dot(flat(e[...]), flat(cols[:, d]), ((0,), (0,)))
        side = term if side is None else side + term
    side = (0.5 * side + kept[wa:]).astype(BF16)
    for a, j, lo in ((a0, 0, 0), (a1, 1, 0), (a2, 2, 0), (a2b, 2, 2), (a3, 3, 0)):
        n = a.shape[0]
        upper = dot(flat(a[:, :rows]), main, ((1,), (0,)))
        for z in range(n):
            e = (e0, e1, e2, e3)[lo + z]
            out[j, lo + z] = upper[z * rows : (z + 1) * rows] + dot(e[j, :rows], side, ((1,), (0,)))


def flat(value):
    return value.reshape(-1, value.shape[-1])


def call(kernel, shape, flops, *args):
    spec = pl.BlockSpec(memory_space=pltpu.VMEM)
    size = sum(a.size * a.dtype.itemsize for a in args)
    return pl.pallas_call(
        kernel,
        out_shape=jax.ShapeDtypeStruct(shape, F32),
        in_specs=[spec] * len(args),
        out_specs=spec,
        compiler_params=pltpu.CompilerParams(vmem_limit_bytes=48 << 20),
        cost_estimate=pl.CostEstimate(flops=flops, bytes_accessed=size, transcendentals=0),
    )(*args)


def body(orbitals, gradient, stored):
    k, n = orbitals.shape
    rows, w, hw = 2 * k, n // 16, n // 32
    wa = 3 * w // 4
    core, zl, y = (lax.axis_index(a) for a in ("core", "zl", "y"))

    own = jnp.stack([orbitals, gradient])
    sibling = shift(own, "core", 1)
    both = jnp.where(core == 0, jnp.concatenate([own, sibling], 1), jnp.concatenate([sibling, own], 1))

    to_r = pick(both.reshape(2, rows, 2, 4, 2, w), core, 4).transpose(3, 2, 0, 1, 4)
    to_c = pick(both[::-1].reshape(2, rows, 4, 4, 2, hw), core, 4).transpose(2, 3, 0, 1, 4)

    part_r = exchange(to_r, "x", 0)
    part_r = exchange(part_r, "zh", 1).transpose(2, 0, 1, 3, 4).reshape(16 * rows, w)
    part_c = exchange(to_c, "zl", 0)
    part_c = jnp.stack(gather(part_c, "zh"))
    part_c = exchange(part_c, "y", 2)

    near = jnp.stack(gather(part_r[:, :wa], "zl"))
    edge = jnp.stack(gather(part_r[:, wa:], "y"))
    a0, a1, a2, a2b, a3 = gather_ring(near, "y")
    edges = gather(edge, "zl")

    c0, c1, c2, c2b, c3 = gather_ring(part_c, "x")
    panel = jnp.stack([c0, c1, jnp.concatenate([c2, c2b]), c3])
    panel = panel.transpose(1, 3, 4, 2, 0, 5, 6).reshape(4, 4, 16 * rows, hw)
    other = shift(panel, "core", 1)

    def share(cols, which):
        kept = lax.dynamic_slice_in_dim(stored, which * hw, hw, 1)
        early = call(early_kernel, (wa, hw), 2 * 192 * rows * wa * hw, a0, a1, a3, cols)
        flops = 2 * 64 * rows * (wa + 4 * (w - wa)) * hw + 2 * 128 * rows * w * hw
        return call(share_kernel, (4, 4, 8 * rows, hw), flops, a0, a1, a2, a2b, a3, *edges, cols, early, kept)

    away = shift(share(other, 1 - core), "core", 1)
    total = (share(panel, core) + away).reshape(16, 2, 4, rows, hw)

    got = [shift(total[:, :, 4 - d].astype(BF16), "x", d) for d in range(1, 4)]
    total = total[:, :, 0] + sum(g.astype(F32) for g in got)
    total = total[:, 0] + shift(total[:, 1].astype(BF16), "zh", 1).astype(F32)

    mine = part_c[:, 0, :, 0].reshape(16, rows, hw).astype(F32)
    result = (mine - total).astype(BF16).reshape(4, 4, rows, hw)
    back = result[::-1, ::-1]
    back = lax.dynamic_slice_in_dim(jnp.concatenate([back, back], 0), 3 - y, 4, 0)
    back = lax.dynamic_slice_in_dim(jnp.concatenate([back, back], 1), 3 - zl, 4, 1)
    result = lax.all_to_all(
        back.transpose(1, 0, 2, 3).reshape(16, rows, hw), ("zl", "y"), split_axis=0, concat_axis=0, tiled=True
    )
    result = result.reshape(16, 2, k, hw)
    kept, got = pick(result, core, 1), shift(pick(result, 1 - core, 1), "core", 1)
    halves = jnp.where(core == 0, jnp.stack([kept, got]), jnp.stack([got, kept]))
    return halves.transpose(2, 1, 0, 3).reshape(k, n)


def solution(mesh):
    fine = Mesh(mesh.devices.reshape(tuple(SIZES.values())), AXES)
    return jax.shard_map(
        body,
        mesh=fine,
        in_specs=(P(AXES, None), P(AXES, None), P(("zh", "x", "core"), ("zl", "y"))),
        out_specs=P(AXES, None),
        check_vma=False,
    )
```

```python
import jax
import jax.numpy as jnp
from jax import lax
from jax.experimental import pallas as pl
from jax.experimental.pallas import tpu as pltpu
from jax.sharding import Mesh, PartitionSpec as P

AXES = ("zh", "x", "core", "zl", "y")
SIZES = {"zh": 2, "x": 4, "core": 2, "zl": 4, "y": 4}
F32, BF16 = jnp.float32, jnp.bfloat16


def shift(value, axis, step):
    n = SIZES[axis]
    return lax.ppermute(value, axis, [(i, (i + step) % n) for i in range(n)])


def pick(value, index, dim=0):
    return lax.dynamic_index_in_dim(value, index, dim, keepdims=False)


def exchange(pieces, axis, dim):
    n = SIZES[axis]
    me = lax.axis_index(axis)
    sent = [pick(pieces, (me + d) % n, dim) for d in range(n)]
    return jnp.stack([sent[0]] + [shift(sent[d], axis, d) for d in range(1, n)])


def gather(block, axis):
    return [block] + [shift(block, axis, d) for d in range(1, SIZES[axis])]


def gather_ring(block, axis):
    half = block.shape[0] // 2
    left, right = shift(block, axis, 1), shift(block, axis, -1)
    return block, left, shift(left[:half], axis, 1), shift(right[half:], axis, -1), right


def dot(left, right, dims):
    return lax.dot_general(left, right, (dims, ((), ())), preferred_element_type=F32)


def early_kernel(a0, a1, a3, cols, out):
    total = None
    for a, j in ((a0, 0), (a1, 1), (a3, 3)):
        term = dot(flat(a[...]), flat(cols[j]), ((0,), (0,)))
        total = term if total is None else total + term
    out[...] = total


def share_kernel(which, a0, a1, a2, a2b, a3, e0, e1, e2, e3, cols, early, stored, out, kept, tile, sem):
    wa, hw = early.shape
    rows = a0.shape[1] // 2
    edges = (e0, e1, e2, e3)
    start = pl.multiple_of(which[0] * hw, hw)
    load = pltpu.make_async_copy(stored.at[:, pl.ds(start, hw)], kept, sem)
    load.start()
    side = None
    for d, e in enumerate(edges):
        term = dot(flat(e[...]), flat(cols[:, d]), ((0,), (0,)))
        side = term if side is None else side + term
    main = early[...]
    main += dot(flat(a2[...]), flat(cols[2, :2]), ((0,), (0,)))
    main += dot(flat(a2b[...]), flat(cols[2, 2:]), ((0,), (0,)))
    load.wait()
    tile[:wa] = (0.5 * main + kept[:wa]).astype(BF16)
    tile[wa:] = (0.5 * side + kept[wa:]).astype(BF16)
    for a, j, lo in ((a0, 0, 0), (a1, 1, 0), (a2, 2, 0), (a2b, 2, 2), (a3, 3, 0)):
        n = a.shape[0]
        wide = flat(a[:, :rows])
        thin = jnp.concatenate([edges[lo + z][j, :rows] for z in range(n)])
        value = dot(jnp.concatenate([wide, thin], 1), tile[...], ((1,), (0,)))
        out[j, lo : lo + n] = value.reshape(n, rows, hw)


def flat(value):
    return value.reshape(-1, value.shape[-1])


VMEM_SPEC = pl.BlockSpec(memory_space=pltpu.VMEM)


def call(kernel, shape, flops, args, specs, scratch=()):
    size = sum(a.size * a.dtype.itemsize for a in args)
    return pl.pallas_call(
        kernel,
        out_shape=jax.ShapeDtypeStruct(shape, F32),
        in_specs=specs,
        out_specs=VMEM_SPEC,
        scratch_shapes=scratch,
        compiler_params=pltpu.CompilerParams(vmem_limit_bytes=48 << 20),
        cost_estimate=pl.CostEstimate(flops=flops, bytes_accessed=size, transcendentals=0),
    )(*args)


def body(orbitals, gradient, stored):
    k, n = orbitals.shape
    rows, w, hw = 2 * k, n // 16, n // 32
    wa = 3 * w // 4
    core, zl, y = (lax.axis_index(a) for a in ("core", "zl", "y"))

    near, far = (orbitals, gradient), [shift(v, "core", 1) for v in (orbitals, gradient)]
    both = jnp.stack([jnp.where(core == 0, jnp.concatenate([p, q]), jnp.concatenate([q, p])) for p, q in zip(near, far)])

    to_r = pick(both.reshape(2, rows, 2, 4, 2, w), core, 4).transpose(3, 2, 0, 1, 4)
    to_c = pick(both[::-1].reshape(2, rows, 4, 4, 2, hw), core, 4).transpose(2, 3, 0, 1, 4)

    part_r = exchange(to_r, "x", 0)
    part_r = exchange(part_r, "zh", 1).transpose(2, 0, 1, 3, 4).reshape(16 * rows, w)
    part_c = exchange(to_c, "zl", 0)
    part_c = exchange(part_c, "y", 1)
    mine = part_c[:, :, 0].reshape(16, rows, hw).astype(F32)
    part_c = jnp.stack(gather(part_c, "zh"), 1)

    near = jnp.stack(gather(part_r[:, :wa], "zl"))
    edge = jnp.stack(gather(part_r[:, wa:], "y"))
    a0, a1, a2, a2b, a3 = gather_ring(near, "y")
    edges = gather(edge, "zl")

    c0, c1, c2, c2b, c3 = gather_ring(part_c, "x")
    panel = jnp.stack([c0, c1, jnp.concatenate([c2, c2b]), c3])
    panel = panel.transpose(1, 3, 4, 2, 0, 5, 6).reshape(4, 4, 16 * rows, hw)
    other = shift(panel, "core", 1)

    def share(cols, which):
        early = call(early_kernel, (wa, hw), 2 * 192 * rows * wa * hw, (a0, a1, a3, cols), [VMEM_SPEC] * 4)
        flops = 2 * 64 * rows * (wa + 4 * (w - wa)) * hw + 2 * 128 * rows * w * hw
        args = (which[None], a0, a1, a2, a2b, a3, *edges, cols, early, stored)
        specs = [pl.BlockSpec(memory_space=pltpu.SMEM)] + [VMEM_SPEC] * 11 + [pl.BlockSpec(memory_space=pl.ANY)]
        scratch = (pltpu.VMEM((w, hw), F32), pltpu.VMEM((w, hw), BF16), pltpu.SemaphoreType.DMA)
        return call(share_kernel, (4, 4, 8 * rows, hw), flops, args, specs, scratch)

    away = shift(share(other, 1 - core), "core", 1)
    total = (share(panel, core) + away).reshape(16, 2, 4, rows, hw)

    got = [shift(total[:, :, 4 - d].astype(BF16), "x", d) for d in range(1, 4)]
    total = total[:, :, 0] + sum(g.astype(F32) for g in got)
    total = total[:, 0] + shift(total[:, 1], "zh", 1)

    result = (mine - total).astype(BF16).reshape(4, 4, rows, hw)
    back = result[::-1, ::-1]
    back = lax.dynamic_slice_in_dim(jnp.concatenate([back, back], 0), 3 - y, 4, 0)
    back = lax.dynamic_slice_in_dim(jnp.concatenate([back, back], 1), 3 - zl, 4, 1)
    result = lax.all_to_all(
        back.transpose(1, 0, 2, 3).reshape(16, rows, hw), ("zl", "y"), split_axis=0, concat_axis=0, tiled=True
    )
    result = result.reshape(16, 2, k, hw)
    kept, got = pick(result, core, 1), shift(pick(result, 1 - core, 1), "core", 1)
    halves = jnp.where(core == 0, jnp.stack([kept, got]), jnp.stack([got, kept]))
    return halves.transpose(2, 1, 0, 3).reshape(k, n)


def solution(mesh):
    fine = Mesh(mesh.devices.reshape(tuple(SIZES.values())), AXES)
    return jax.shard_map(
        body,
        mesh=fine,
        in_specs=(P(AXES, None), P(AXES, None), P(("zh", "x", "core"), ("zl", "y"))),
        out_specs=P(AXES, None),
        check_vma=False,
    )
```

```python
import jax
import jax.numpy as jnp
from jax import lax
from jax.experimental import pallas as pl
from jax.experimental.pallas import tpu as pltpu
from jax.sharding import Mesh, PartitionSpec as P

AXES = ("zh", "x", "core", "zl", "y")
SIZES = {"zh": 2, "x": 4, "core": 2, "zl": 4, "y": 4}
F32, BF16 = jnp.float32, jnp.bfloat16


def shift(value, axis, step):
    n = SIZES[axis]
    return lax.ppermute(value, axis, [(i, (i + step) % n) for i in range(n)])


def pick(value, index, dim=0):
    return lax.dynamic_index_in_dim(value, index, dim, keepdims=False)


def exchange(pieces, axis, dim):
    n = SIZES[axis]
    me = lax.axis_index(axis)
    sent = [pick(pieces, (me + d) % n, dim) for d in range(n)]
    return jnp.stack([sent[0]] + [shift(sent[d], axis, d) for d in range(1, n)])


def gather(block, axis):
    return [block] + [shift(block, axis, d) for d in range(1, SIZES[axis])]


def gather_ring(block, axis):
    half = block.shape[0] // 2
    left, right = shift(block, axis, 1), shift(block, axis, -1)
    return block, left, shift(left[:half], axis, 1), shift(right[half:], axis, -1), right


def absolute(pieces, me, n, dim):
    turned = jnp.flip(pieces, dim)
    twice = jnp.concatenate([turned, turned], dim)
    return lax.dynamic_slice_in_dim(twice, n - 1 - me, n, dim)


def dot(left, right, dims):
    return lax.dot_general(left, right, (dims, ((), ())), preferred_element_type=F32)


def pair_kernel(a0, a1, a2, a2b, a3, part, out):
    for a, j, lo in ((a0, 0, 0), (a1, 1, 0), (a2, 2, 0), (a2b, 2, 2), (a3, 3, 0)):
        n = a.shape[0]
        value = dot(flat(a[...]), part[...], ((1,), (1,)))
        out[j, lo : lo + n] = value.reshape(n, a.shape[1], -1)


def tile_kernel(which, x_ref, kept, out, tile):
    @pl.when(pl.program_id(0) == 0)
    def _():
        tile[...] = kept[...].astype(BF16)

    out[...] = dot(x_ref[...], tile[...], ((1,), (0,)))


def mix_kernel(pairs, panel, tiles, mine, out, total):
    n = panel.shape[0]
    total[...] = jnp.zeros_like(total)

    @pl.loop(0, n * n)
    def _(step):
        dy, dz = step // n, step % n
        rows = []
        for i in range(n):
            src = (i + n - dy) % n
            rows += [pairs[src // 2, dy, dz, src % 2, (j + n - dz) % n] for j in range(n)]
        value = jnp.concatenate(rows)
        high = value.astype(BF16)
        low = (value - high.astype(F32)).astype(BF16)
        right = panel[dy, dz]
        total[...] += dot(jnp.concatenate([high, low], 1), jnp.concatenate([right, right]), ((1,), (0,)))

    out[...] = (mine[...].astype(F32) - (0.5 * total[...] + tiles[...])).astype(BF16)


def flat(value):
    return value.reshape(-1, value.shape[-1])


VMEM_SPEC = pl.BlockSpec(memory_space=pltpu.VMEM)


def call(kernel, shape, flops, args, specs, scratch=(), kind=F32):
    size = sum(a.size * a.dtype.itemsize for a in args)
    return pl.pallas_call(
        kernel,
        out_shape=jax.ShapeDtypeStruct(shape, kind),
        in_specs=specs,
        out_specs=VMEM_SPEC,
        scratch_shapes=scratch,
        compiler_params=pltpu.CompilerParams(vmem_limit_bytes=48 << 20),
        cost_estimate=pl.CostEstimate(flops=flops, bytes_accessed=size, transcendentals=0),
    )(*args)


def body(orbitals, gradient, stored):
    k, n = orbitals.shape
    rows, w, hw = 2 * k, n // 16, n // 32
    zh, x, core, zl, y = (lax.axis_index(a) for a in AXES)

    near, far = (orbitals, gradient), [shift(v, "core", 1) for v in (orbitals, gradient)]
    both = jnp.stack([jnp.where(core == 0, jnp.concatenate([p, q]), jnp.concatenate([q, p])) for p, q in zip(near, far)])

    to_r = pick(both.reshape(2, rows, 2, 4, 2, w), core, 4).transpose(3, 2, 0, 1, 4)
    to_c = pick(both[::-1].reshape(2, rows, 4, 4, 2, hw), core, 4).transpose(2, 3, 0, 1, 4)

    part_r = exchange(to_r, "x", 0)
    part_r = exchange(part_r, "zh", 1)
    near = jnp.stack(gather(part_r[:, :, 0].reshape(8 * rows, w), "zl"))
    pieces = gather_ring(near, "y")
    ordered = absolute(absolute(part_r, zh, 2, 0), x, 4, 1)
    ordered = ordered.transpose(2, 0, 1, 3, 4).reshape(16 * rows, w)

    part_c = exchange(to_c, "zl", 0)
    part_c = lax.optimization_barrier(exchange(part_c, "y", 1))
    mine = part_c[:, :, 0].reshape(16 * rows, hw)
    parts = gather(part_c, "zh")
    part_c = absolute(jnp.stack(parts), zh, 2, 0).transpose(1, 0, 2, 3, 4, 5)
    c0, c1, c2, c2b, c3 = gather_ring(part_c, "x")
    panel = absolute(jnp.stack([c0, c1, jnp.concatenate([c2, c2b]), c3]), x, 4, 0)
    panel = panel.transpose(1, 3, 4, 2, 0, 5, 6).reshape(4, 4, 16 * rows, hw)

    pairs = call(
        pair_kernel, (4, 4, 8 * rows, 16 * rows), 2 * 128 * rows * 16 * rows * w, (*pieces, ordered), [VMEM_SPEC] * 6
    ).reshape(2, 2, 4, 2, 4, rows, 16 * rows)
    pairs = pick(pairs, core) + shift(pick(pairs, 1 - core), "core", 1)
    pairs = pairs[:, :, :, 0] + sum(shift(pairs[:, :, :, 4 - d], "x", d) for d in range(1, 4))
    pairs = pairs[:, :, 0] + shift(pairs[:, :, 1], "zh", 1)
    pairs = jnp.stack(gather(pairs, "zl"))
    pairs = jnp.stack(gather(pairs, "y"))
    twin = shift(pairs, "core", 1)
    pairs = jnp.where(core == 0, jnp.stack([pairs, twin]), jnp.stack([twin, pairs]))

    x_r = jnp.concatenate([flat(p) for p in pieces])

    def product(which):
        step = 32 * rows
        grid = pltpu.PrefetchScalarGridSpec(
            num_scalar_prefetch=1,
            grid=(4,),
            in_specs=[pl.BlockSpec((step, w), lambda i, s: (i, 0)), pl.BlockSpec((w, hw), lambda i, s: (0, s[0]))],
            out_specs=pl.BlockSpec((step, hw), lambda i, s: (i, 0)),
            scratch_shapes=[pltpu.VMEM((w, hw), BF16)],
        )
        return pl.pallas_call(
            tile_kernel,
            out_shape=jax.ShapeDtypeStruct((4 * step, hw), F32),
            grid_spec=grid,
            compiler_params=pltpu.CompilerParams(vmem_limit_bytes=32 << 20),
            cost_estimate=pl.CostEstimate(flops=8 * step * w * hw, bytes_accessed=6 * w * hw, transcendentals=0),
        )(which[None], x_r, stored)

    away = product(1 - core)
    away = shift(away, "core", 1)
    own = product(core)
    total = (own + away).reshape(16, 2, 4, rows, hw)
    sent = [total[:, :, 4 - d].astype(BF16) for d in range(1, 4)]
    got = [shift(v, "x", d) for d, v in enumerate(sent, 1)]
    total = total[:, :, 0] + sum(g.astype(F32) for g in got)
    total = total[:, 0] + shift(total[:, 1].astype(BF16), "zh", 1).astype(F32)

    args = (pairs, panel, total.reshape(16 * rows, hw), mine)
    result = call(mix_kernel, mine.shape, 8 * 16 * rows * 128 * rows * hw, args, [VMEM_SPEC] * 4, [pltpu.VMEM(mine.shape, F32)], BF16)
    result = result.reshape(4, 4, rows, hw)
    back = absolute(absolute(result, y, 4, 0), zl, 4, 1)
    result = lax.all_to_all(
        back.transpose(1, 0, 2, 3).reshape(16, rows, hw), ("zl", "y"), split_axis=0, concat_axis=0, tiled=True
    )
    result = result.reshape(16, 2, k, hw)
    kept, got = pick(result, core, 1), shift(pick(result, 1 - core, 1), "core", 1)
    halves = jnp.where(core == 0, jnp.stack([kept, got]), jnp.stack([got, kept]))
    return halves.transpose(2, 1, 0, 3).reshape(k, n)


def solution(mesh):
    fine = Mesh(mesh.devices.reshape(tuple(SIZES.values())), AXES)
    return jax.shard_map(
        body,
        mesh=fine,
        in_specs=(P(AXES, None), P(AXES, None), P(("zh", "x", "core"), ("zl", "y"))),
        out_specs=P(AXES, None),
        check_vma=False,
    )
```

```python
import jax
import jax.numpy as jnp
from jax import lax
from jax.experimental import pallas as pl
from jax.experimental.pallas import tpu as pltpu
from jax.sharding import Mesh, PartitionSpec as P

AXES = ("zh", "x", "core", "zl", "y")
SIZES = {"zh": 2, "x": 4, "core": 2, "zl": 4, "y": 4}
F32, BF16 = jnp.float32, jnp.bfloat16


def shift(value, axis, step):
    n = SIZES[axis]
    return lax.ppermute(value, axis, [(i, (i + step) % n) for i in range(n)])


def pick(value, index, dim=0):
    return lax.dynamic_index_in_dim(value, index, dim, keepdims=False)


def exchange(pieces, axis, dim):
    n = SIZES[axis]
    me = lax.axis_index(axis)
    sent = [pick(pieces, (me + d) % n, dim) for d in range(n)]
    return jnp.stack([sent[0]] + [shift(sent[d], axis, d) for d in range(1, n)])


def gather(block, axis):
    return [block] + [shift(block, axis, d) for d in range(1, SIZES[axis])]


def gather_ring(block, axis):
    half = block.shape[0] // 2
    left, right = shift(block, axis, 1), shift(block, axis, -1)
    return block, left, shift(left[:half], axis, 1), shift(right[half:], axis, -1), right


def absolute(pieces, me, n, dim):
    turned = jnp.flip(pieces, dim)
    twice = jnp.concatenate([turned, turned], dim)
    return lax.dynamic_slice_in_dim(twice, n - 1 - me, n, dim)


def dot(left, right, dims):
    return lax.dot_general(left, right, (dims, ((), ())), preferred_element_type=F32)


def pair_kernel(a0, a1, a2, a2b, a3, part, out):
    for a, j, lo in ((a0, 0, 0), (a1, 1, 0), (a2, 2, 0), (a2b, 2, 2), (a3, 3, 0)):
        n = a.shape[0]
        value = dot(flat(a[...]), part[...], ((1,), (1,)))
        out[j, lo : lo + n] = value.reshape(n, a.shape[1], -1)


def tile_kernel(which, x_ref, kept, out, tile):
    @pl.when(pl.program_id(0) == 0)
    def _():
        tile[...] = kept[...].astype(BF16)

    out[...] = dot(x_ref[...], tile[...], ((1,), (0,)))


def mix_kernel(core, mine_pairs, twin_pairs, panel, near, far, mine, out, total):
    n = panel.shape[0]
    total[...] = jnp.zeros_like(total)

    @pl.loop(0, n * n)
    def _(step):
        dy, dz = step // n, step % n
        rows = []
        for i in range(n):
            src = (i + n - dy) % n
            held = src // 2 == core[0]
            for j in range(n):
                at = (dy, dz, src % 2, (j + n - dz) % n)
                rows.append(jnp.where(held, mine_pairs[at], twin_pairs[at]))
        value = jnp.concatenate(rows)
        high = value.astype(BF16)
        low = (value - high.astype(F32)).astype(BF16)
        right = panel[dy, dz]
        total[...] += dot(jnp.concatenate([high, low], 1), jnp.concatenate([right, right]), ((1,), (0,)))

    out[...] = (mine[...].astype(F32) - (0.5 * total[...] + (near[...] + far[...].astype(F32)))).astype(BF16)


def flat(value):
    return value.reshape(-1, value.shape[-1])


VMEM_SPEC = pl.BlockSpec(memory_space=pltpu.VMEM)


def call(kernel, shape, flops, args, specs, scratch=(), kind=F32):
    size = sum(a.size * a.dtype.itemsize for a in args)
    return pl.pallas_call(
        kernel,
        out_shape=jax.ShapeDtypeStruct(shape, kind),
        in_specs=specs,
        out_specs=VMEM_SPEC,
        scratch_shapes=scratch,
        compiler_params=pltpu.CompilerParams(vmem_limit_bytes=48 << 20),
        cost_estimate=pl.CostEstimate(flops=flops, bytes_accessed=size, transcendentals=0),
    )(*args)


def body(orbitals, gradient, stored):
    k, n = orbitals.shape
    rows, w, hw = 2 * k, n // 16, n // 32
    zh, x, core, zl, y = (lax.axis_index(a) for a in AXES)

    near, far = (orbitals, gradient), [shift(v, "core", 1) for v in (orbitals, gradient)]
    both = jnp.stack([jnp.where(core == 0, jnp.concatenate([p, q]), jnp.concatenate([q, p])) for p, q in zip(near, far)])

    to_r = pick(both.reshape(2, rows, 2, 4, 2, w), core, 4).transpose(3, 2, 0, 1, 4)
    to_c = pick(both[::-1].reshape(2, rows, 4, 4, 2, hw), core, 4).transpose(2, 3, 0, 1, 4)

    part_r = exchange(to_r, "x", 0)
    part_r = exchange(part_r, "zh", 1)
    near = jnp.stack(gather(part_r[:, :, 0].reshape(8 * rows, w), "zl"))
    pieces = gather_ring(near, "y")
    ordered = absolute(absolute(part_r, zh, 2, 0), x, 4, 1)
    ordered = ordered.transpose(2, 0, 1, 3, 4).reshape(16 * rows, w)

    part_c = exchange(to_c, "zl", 0)
    part_c = lax.optimization_barrier(exchange(part_c, "y", 1))
    mine = part_c[:, :, 0].reshape(16 * rows, hw)
    parts = gather(part_c, "zh")
    part_c = absolute(jnp.stack(parts), zh, 2, 0).transpose(1, 0, 2, 3, 4, 5)
    part_c = lax.optimization_barrier(part_c)
    c0, c1, c2, c2b, c3 = gather_ring(part_c, "x")
    panel = absolute(jnp.stack([c0, c1, jnp.concatenate([c2, c2b]), c3]), x, 4, 0)
    panel = panel.transpose(1, 3, 4, 2, 0, 5, 6).reshape(4, 4, 16 * rows, hw)

    pairs = call(
        pair_kernel, (4, 4, 8 * rows, 16 * rows), 2 * 128 * rows * 16 * rows * w, (*pieces, ordered), [VMEM_SPEC] * 6
    ).reshape(2, 2, 4, 2, 4, rows, 16 * rows)
    pairs = pick(pairs, core) + shift(pick(pairs, 1 - core), "core", 1)
    pairs = pairs[:, :, :, 0] + sum(shift(pairs[:, :, :, 4 - d], "x", d) for d in range(1, 4))
    pairs = pairs[:, :, 0] + shift(pairs[:, :, 1], "zh", 1)
    pairs = jnp.stack(gather(pairs, "zl"))
    pairs = jnp.stack(gather(pairs, "y"))
    twin = shift(pairs, "core", 1)

    x_r = jnp.concatenate([flat(p) for p in pieces])

    def product(which):
        step = 32 * rows
        grid = pltpu.PrefetchScalarGridSpec(
            num_scalar_prefetch=1,
            grid=(4,),
            in_specs=[pl.BlockSpec((step, w), lambda i, s: (i, 0)), pl.BlockSpec((w, hw), lambda i, s: (0, s[0]))],
            out_specs=pl.BlockSpec((step, hw), lambda i, s: (i, 0)),
            scratch_shapes=[pltpu.VMEM((w, hw), BF16)],
        )
        return pl.pallas_call(
            tile_kernel,
            out_shape=jax.ShapeDtypeStruct((4 * step, hw), F32),
            grid_spec=grid,
            compiler_params=pltpu.CompilerParams(vmem_limit_bytes=32 << 20),
            cost_estimate=pl.CostEstimate(flops=8 * step * w * hw, bytes_accessed=6 * w * hw, transcendentals=0),
        )(which[None], x_r, stored)

    away = product(1 - core)
    away = shift(away, "core", 1)
    own = product(core)
    total = (own + away).reshape(16, 2, 4, rows, hw)
    sent = [total[:, :, 4 - d].astype(BF16) for d in range(1, 4)]
    got = [shift(v, "x", d) for d, v in enumerate(sent, 1)]
    total = total[:, :, 0] + sum(g.astype(F32) for g in got)
    sent = total[:, 1].astype(BF16)
    got = shift(sent, "zh", 1)

    args = (core[None], pairs, twin, panel, flat(total[:, 0]), flat(got), mine)
    specs = [pl.BlockSpec(memory_space=pltpu.SMEM)] + [VMEM_SPEC] * 6
    flops = 8 * 16 * rows * 128 * rows * hw
    result = call(mix_kernel, mine.shape, flops, args, specs, [pltpu.VMEM(mine.shape, F32)], BF16)
    result = result.reshape(4, 4, rows, hw)
    back = absolute(absolute(result, y, 4, 0), zl, 4, 1)
    result = lax.all_to_all(
        back.transpose(1, 0, 2, 3).reshape(16, rows, hw), ("zl", "y"), split_axis=0, concat_axis=0, tiled=True
    )
    result = result.reshape(16, 2, k, hw)
    kept, got = pick(result, core, 1), shift(pick(result, 1 - core, 1), "core", 1)
    halves = jnp.where(core == 0, jnp.stack([kept, got]), jnp.stack([got, kept]))
    return halves.transpose(2, 1, 0, 3).reshape(k, n)


def solution(mesh):
    fine = Mesh(mesh.devices.reshape(tuple(SIZES.values())), AXES)
    return jax.shard_map(
        body,
        mesh=fine,
        in_specs=(P(AXES, None), P(AXES, None), P(("zh", "x", "core"), ("zl", "y"))),
        out_specs=P(AXES, None),
        check_vma=False,
    )
```
